32 devices in a mesh: groups: 2 (over x), expert: 8 (over z, y), wave: 2 (over core).
Axes of the slice: x: 2, y: 2, z: 4, core: 2. Of those that a mesh axis runs over, the one named last changes fastest.
Arguments:
- hidden_rows: bfloat16 [512, 2, 2048], P(('groups', 'expert', 'wave')), parts along dimension 0, may hold values from -6 to 6
- expert_ids: int32 [512, 2, 8], P(('groups', 'expert', 'wave')), parts along dimension 0, may hold values from 0 to 15, all different within a row; in each aligned block of 32 rows (0 to 31, 32 to 63, ..., all dimensions but the last counted through in order) at most 24 rows name the same one
- route_weights: float32 [512, 2, 8], P(('groups', 'expert', 'wave')), parts along dimension 0, may hold values from 0.1 to 1
- w_gate: bfloat16 [16, 2048, 768], P('expert', None, 'wave'), may hold values from -0.125 to 0.125
- w_up: bfloat16 [16, 2048, 768], P('expert', None, 'wave'), may hold values from -0.125 to 0.125
- w_down: bfloat16 [16, 768, 2048], P('expert', 'wave'), may hold values from -0.21875 to 0.21875
- codes: int32 [512, 2, 16], P(('groups', 'expert', 'wave')), parts along dimension 0, may hold values from 0 to 1023
- owner_slot: int32 [512], P(('groups', 'expert', 'wave')), parts along dimension 0, may hold values from 0 to 255, as said below
- code_table: bfloat16 [16, 1024, 1024], P(None, 'expert'), may hold values from -1.5 to 1.5
- conv_state: bfloat16 [512, 6, 1024], P(('groups', 'expert', 'wave')), parts along dimension 0, may hold values from -6 to 6
- conv_taps: float32 [7, 1024], replicated, may hold values from -2.4 to 2.4
- conv_bias: float32 [1024], replicated, may hold values from -3 to 3
- upsample: bfloat16 [1024, 512], replicated, may hold values from -0.1875 to 0.1875
Outputs:
- moe_out: bfloat16 [512, 2, 2048], P(('groups', 'expert', 'wave')), parts along dimension 0
- waveform: bfloat16 [512, 2, 512], P(('groups', 'expert', 'wave')), parts along dimension 0
- new_state: bfloat16 [512, 6, 1024], P(('groups', 'expert', 'wave')), parts along dimension 0
The draws below stay inside these ranges and needn't reach their ends.
There are 2 independent parts, one for each index of `groups`. The reference program is written for one: setup_inputs(seed, part) draws one part's arguments, and reference() takes and returns one part's arrays. A program takes and returns all parts, laid end to end along the dimension named above; an argument that names none is the same for every part. Nothing has to cross between parts.
Inputs may be any that keep to these rules, and one draw needn't show every extreme that they name: `expert_ids`: each row names 8 different experts; among the 32 rows of one device no expert is named more than 24 times, a bound that some block reaches. `owner_slot`: A permutation of the slots. Slot o lies on the device holding rows o of the decoder's arrays; a session's slot lies on a device with the same index along wave as the session's own device, so every device holds 16 slots.
All inputs are finite; a program needn't handle non-finite values.
Results may differ from the reference program's by a relative error of at most 0.012.
Values may be sent and summed in bfloat16 or wider, within the bound.
A program may use at most 64 MiB of HBM per device.

```python
import math
import jax
import jax.numpy as jnp
import numpy as np
from jax import lax

D = 2048
FF = 768
TOP = 8
STEPS = 2
SESS_DEV = 16
CODEBOOKS = 16
CODES = 1024
DC = 1024
KERNEL = 7
UP = 2
OUT_CH = 256
EXPERTS = 16
CAP = 24
SESSIONS = 256
STATE = 6
N_EXPERT = 8
N_WAVE = 2


def draw_owner_slot(key, part):
    count = SESSIONS // N_WAVE
    owners = jnp.zeros((SESSIONS,), jnp.int32)
    within = jnp.arange(count, dtype=jnp.int32)
    for wave_index in range(N_WAVE):
        order = jax.random.permutation(jax.random.fold_in(key, 11 + wave_index), count).astype(jnp.int32)
        where = (within // SESS_DEV * N_WAVE + wave_index) * SESS_DEV + within % SESS_DEV
        target = (order // SESS_DEV * N_WAVE + wave_index) * SESS_DEV + order % SESS_DEV
        owners = owners.at[where].set(target)
    return owners


def place_ends(values, rng, smallest, largest):
    extent = values.shape
    place = [jax.random.randint(jax.random.fold_in(rng, axis), (), 0, extent[axis]) for axis in range(len(extent))]
    values = values.at[tuple(place)].set(smallest)
    longest = extent.index(max(extent))
    place[longest] = (place[longest] + 1) % extent[longest]
    return values.at[tuple(place)].set(largest)


def block_scale(own_key, dims, shards, least, top_value):
    level = 1.0
    for dim, parts in shards:
        draws = jax.random.uniform(jax.random.fold_in(jax.random.fold_in(own_key, 6), dim), (parts,), jnp.float32, least / len(shards), top_value / len(shards))
        level = level * jnp.repeat(jnp.exp(draws), dims[dim] // parts).reshape((-1,) + (1,) * (len(dims) - 1 - dim))
    return level


def shared_out(rng, own, number, rows, amount, top, limit, lean):
    sequence = jax.random.permutation(rng, amount)
    crowded, ordinary = shares(amount, rows * top, limit, lean, True), shares(amount, rows * top, limit, lean, False)
    places = jnp.arange(amount)

    def named(sizes, offset_by):
        used = int((sizes > 0).sum())
        fixed = max(1, used // 4)
        passed = fixed + (places - fixed + offset_by * (used - fixed)) % max(1, amount - fixed)
        return jnp.zeros((amount,), jnp.int32).at[sequence[jnp.where(places < fixed, places, passed)]].set(jnp.asarray(sizes, jnp.int32))

    sizes = jnp.where(number % 4 == 0, named(crowded, number // 4), named(ordinary, number - number // 4 - 1))
    mixed = jax.random.permutation(jax.random.fold_in(own, 3), amount)
    source_of, taker = mixed[0:amount // 2 * 2:2], mixed[1:amount // 2 * 2:2]
    room = jnp.minimum(sizes[source_of] - 1, limit - sizes[taker]) // 2
    room = jnp.where((source_of == sequence[0]) | (taker == sequence[0]) | (sizes[taker] == 0), 0, jnp.maximum(room, 0))
    passed = jax.random.randint(jax.random.fold_in(own, 4), (amount // 2,), 0, 1 << 20) % (room + 1)
    sizes = sizes.at[source_of].add(-passed).at[taker].add(passed)
    members = jnp.searchsorted(jnp.cumsum(sizes), jnp.arange(rows * top), side="right").astype(jnp.int32)
    grid = members.reshape(top, rows).T
    grid = grid[jax.random.permutation(jax.random.fold_in(own, 1), rows)]
    offset_by = jax.random.randint(jax.random.fold_in(own, 2), (rows, 1), 0, top)
    return jnp.take_along_axis(grid, (jnp.arange(top)[None, :] + offset_by) % top, axis=1)


def shares(count, total, bound, skew, full):
    portions = [(1 << 20) // math.isqrt(standing ** skew) + 1 for standing in range(1, count + 1)]
    largest = bound if full else min(bound, max(-(-total // count), total * portions[0] // sum(portions)))
    least = 1 if total - largest >= count - 1 else 0
    given, surplus = [largest] + [least] * (count - 1), total - largest - least * (count - 1)
    while surplus > 0:
        movable = [i for i in range(1, count) if given[i] < largest] or [i for i in range(1, count) if given[i] < bound]
        pool, budget = sum([portions[i] for i in movable]), surplus
        for i in movable:
            extra = min(bound - given[i], max(1, budget * portions[i] // pool), surplus)
            given[i] = given[i] + extra
            surplus = surplus - extra
    return np.array(given)


def centred(stream_key, extent, deviation, bound, split=(), held_as=jnp.bfloat16):
    values = jax.random.normal(stream_key, extent, jnp.float32) * deviation
    if len(split) > 0:
        values = block_scale(stream_key, extent, split, -0.22, 0.18) * values
    return jnp.clip(values, min=-bound, max=bound).astype(held_as)


def setup_inputs(seed: int = 0, part: int = 0) -> dict:
    arg_keys = jax.random.split(jax.random.key(seed), 14)
    part_splits = jax.random.split(jax.random.fold_in(arg_keys[13], part), 14)
    hidden_rows = centred(part_splits[0], (SESSIONS, STEPS, D), 1.0, 6.0, ((0, 16),))
    expert_ids_keys = jax.random.split(jax.random.fold_in(part_splits[1], 1), SESSIONS * STEPS // (SESS_DEV * STEPS))
    expert_ids_turns = jax.random.permutation(jax.random.fold_in(part_splits[1], 3), SESSIONS * STEPS // (SESS_DEV * STEPS))
    expert_ids = jax.vmap(lambda own, number: shared_out(jax.random.fold_in(part_splits[1], 2), own, number, SESS_DEV * STEPS, EXPERTS, TOP, CAP, 1))(expert_ids_keys, expert_ids_turns).reshape((SESSIONS, STEPS, TOP))
    route_weights = jnp.clip(jnp.exp(math.log(1.0) - 2.3025851 * jax.random.uniform(part_splits[2], (SESSIONS, STEPS, TOP), jnp.float32) ** block_scale(part_splits[2], (SESSIONS, STEPS, TOP), ((0, 16),), -0.2, 0.2)), 0.1, 1.0)
    w_gate = centred(arg_keys[3], (EXPERTS, D, FF), D ** -0.5, 0.125, ((0, 8), (2, 2)))
    w_up = centred(arg_keys[4], (EXPERTS, D, FF), D ** -0.5, 0.125, ((0, 8), (2, 2)))
    w_down = centred(arg_keys[5], (EXPERTS, FF, D), FF ** -0.5, 0.21875, ((0, 8), (1, 2)))
    codes = place_ends(jax.random.randint(part_splits[6], (SESSIONS, STEPS, CODEBOOKS), 0, CODES), jax.random.fold_in(part_splits[6], 1), 0, CODES - 1).astype(jnp.int32)
    owner_slot = draw_owner_slot(jax.random.fold_in(jax.random.fold_in(arg_keys[13], part), 71), part)
    code_table = centred(arg_keys[8], (CODEBOOKS, CODES, DC), 0.25, 1.5, ((1, 8),))
    conv_state = centred(part_splits[9], (SESSIONS, STATE, DC), 1.0, 6.0, ((0, 16),))
    conv_taps = centred(arg_keys[10], (KERNEL, DC), 0.4, 2.4, (), jnp.float32)
    conv_bias = centred(arg_keys[11], (DC,), 0.5, 3.0, (), jnp.float32)
    upsample = centred(arg_keys[12], (DC, UP * OUT_CH), DC ** -0.5, 0.1875)
    return dict(hidden_rows=hidden_rows, expert_ids=expert_ids, route_weights=route_weights, w_gate=w_gate, w_up=w_up, w_down=w_down, codes=codes, owner_slot=owner_slot, code_table=code_table, conv_state=conv_state, conv_taps=conv_taps, conv_bias=conv_bias, upsample=upsample)


def round_half(value):
    return lax.optimization_barrier(value.astype(jnp.bfloat16)).astype(jnp.float32)


def reference(hidden_rows, expert_ids, route_weights, w_gate, w_up, w_down, codes, owner_slot, code_table, conv_state, conv_taps, conv_bias, upsample):
    row_total = SESSIONS * STEPS
    tok_rows = hidden_rows.reshape(row_total, D)
    chosen = expert_ids.reshape(row_total * TOP).astype(jnp.int32)
    weights_flat = route_weights.reshape(row_total * TOP)
    most = N_EXPERT * N_WAVE * CAP
    group_width = FF // N_WAVE

    def one_expert(total, index):
        hit = chosen == index
        picked = jnp.nonzero(hit, size=most, fill_value=0)[0].astype(jnp.int32)
        valid = (jnp.arange(most, dtype=jnp.int32) < jnp.sum(hit.astype(jnp.int32))).astype(jnp.float32)
        source = picked // TOP
        inputs = tok_rows[source]
        gate_val = jnp.dot(inputs, w_gate[index], preferred_element_type=jnp.float32)
        up_val = jnp.dot(inputs, w_up[index], preferred_element_type=jnp.float32)
        activated = (jax.nn.silu(gate_val) * up_val).astype(jnp.bfloat16)
        down_rows = w_down[index]
        summed = jnp.zeros((most, D), jnp.float32)
        for group in range(N_WAVE):
            term = jnp.dot(activated[:, group * group_width:(group + 1) * group_width], down_rows[group * group_width:(group + 1) * group_width], preferred_element_type=jnp.float32)
            summed = summed + round_half(term)
        slot_out = round_half(summed)
        total = total.at[source].add(slot_out * (weights_flat[picked] * valid)[:, None])
        return total, None

    mixed, _ = lax.scan(one_expert, jnp.zeros((row_total, D), jnp.float32), jnp.arange(EXPERTS, dtype=jnp.int32))
    moe_out = mixed.astype(jnp.bfloat16).reshape(SESSIONS, STEPS, D)

    books = jnp.arange(CODEBOOKS, dtype=jnp.int32)
    looked = code_table[books[None, None, :], codes].astype(jnp.float32)
    frames = jnp.sum(looked, axis=2)
    owned = jnp.zeros((SESSIONS, STEPS, DC), jnp.float32).at[owner_slot].set(frames)
    history = jnp.concatenate([conv_state.astype(jnp.float32), owned], axis=1)
    filtered = jnp.broadcast_to(conv_bias, (SESSIONS, STEPS, DC))
    for offset in range(KERNEL):
        filtered = filtered + conv_taps[offset] * history[:, STATE - offset:STATE - offset + STEPS]
    decoded = jax.nn.gelu(filtered).astype(jnp.bfloat16)
    samples = jnp.dot(decoded.reshape(SESSIONS * STEPS, DC), upsample, preferred_element_type=jnp.float32)
    waveform = samples.astype(jnp.bfloat16).reshape(SESSIONS, STEPS, UP * OUT_CH)
    new_state = history[:, STEPS:].astype(jnp.bfloat16)
    return (moe_out, waveform, new_state)
```

```python
import functools

import jax
import jax.numpy as jnp
from jax import lax
from jax.experimental import pallas as pl
from jax.experimental.pallas import tpu as pltpu
from jax.sharding import PartitionSpec as P

MESH = pl.DeviceIdType.MESH
BF = jnp.bfloat16
F32 = jnp.float32
RADIX = 64
LANES = 128


def dot(a, b):
    return jnp.dot(a, b, preferred_element_type=F32)


def kernel(
    n_e, n_w, inner, experts, books, scales,
    x_ref, wg_ref, wu_ref, wd_ref, tab_ref,
    moe_ref, fr_ref,
    xg, wgu, wdv, tabv, mem, act,
    psend, precv, pown, ps, my, ma, mz,
    fs, fy, fa, fz,
    w_sem, zu_sem, zd_sem, ys_sem, ws_sem, ag_recv,
    p_sem, mys, myr, mzs, mzr, fys, fyr, fzs, fzr,
):
    outer = n_e // inner
    rows = x_ref.shape[0]
    width = moe_ref.shape[1]
    channels = fr_ref.shape[1]
    local = wg_ref.shape[0]
    units = wg_ref.shape[2]
    shard = tab_ref.shape[0] // books
    wave_rows = n_e * rows
    e = lax.axis_index("expert")
    w = lax.axis_index("wave")
    z = e // inner
    y = e % inner
    peer = 1 - w
    ye = z * inner + (inner - 1 - y)

    def remote(src, dst, ssem, rsem, te, tw):
        return pltpu.make_async_remote_copy(
            src_ref=src, dst_ref=dst, send_sem=ssem, recv_sem=rsem,
            device_id={"expert": te, "wave": tw}, device_id_type=MESH,
        )

    loads = []
    loads.append(pltpu.make_async_copy(tab_ref, tabv, w_sem.at[0]))
    for j in range(local):
        loads.append(pltpu.make_async_copy(wg_ref.at[j], wgu.at[j, :, pl.ds(0, units)], w_sem.at[1 + 2 * j]))
        loads.append(pltpu.make_async_copy(wu_ref.at[j], wgu.at[j, :, pl.ds(units, units)], w_sem.at[2 + 2 * j]))
    loads.append(pltpu.make_async_copy(wd_ref, wdv, w_sem.at[1 + 2 * local]))

    barrier = pltpu.get_barrier_semaphore()

    def greet(te, tw):
        pl.semaphore_signal(barrier, inc=1, device_id={"expert": te, "wave": tw}, device_id_type=MESH)

    greet(e, peer)
    if inner == 2:
        greet(ye, w)
    for d in range(1, outer):
        greet((z + d) % outer * inner + y, w)
    pl.semaphore_wait(barrier, 1 + (inner - 1) + (outer - 1))

    def slot(te, tw):
        return xg.at[pl.ds((tw * n_e + te) * rows, rows), :]

    def up(src, zo):
        te = zo * inner + y
        return remote(src, slot(te, w), zu_sem.at[zo], ag_recv.at[w * n_e + te], (z + 1) * inner + y, w)

    def down(src, zo):
        te = zo * inner + y
        return remote(src, slot(te, w), zd_sem.at[zo], ag_recv.at[w * n_e + te], (z - 1) * inner + y, w)

    def across(src, zo):
        te = zo * inner + y
        return remote(src, slot(te, w), ys_sem.at[zo], ag_recv.at[w * n_e + te], ye, w)

    def over(src, te):
        return remote(src, slot(te, w), ws_sem.at[te], ag_recv.at[w * n_e + te], e, peer)

    def arrived(te, tw):
        remote(slot(te, tw), slot(te, tw), ws_sem.at[te], ag_recv.at[tw * n_e + te], e, peer).wait_recv()

    @pl.when(z + 1 < outer)
    def _():
        up(x_ref, z).start()

    @pl.when(z > 0)
    def _():
        down(x_ref, z).start()

    if inner == 2:
        across(x_ref, z).start()
    over(x_ref, e).start()
    for load in loads:
        load.start()
    xg[pl.ds((w * n_e + e) * rows, rows), :] = x_ref[...]

    def spread(zo):
        te = zo * inner + y
        if inner == 2:
            across(slot(te, w), zo).start()
        over(slot(te, w), te).start()

    def from_across(zo):
        te = zo * inner + (inner - 1 - y)
        arrived(te, w)
        over(slot(te, w), te).start()

    def both_sides(step, act_on):
        @pl.when(z - step >= 0)
        def _():
            act_on(z - step)

        @pl.when(z + step < outer)
        def _():
            act_on(z + step)

    for step in range(1, outer):
        @pl.when(z - step >= 0)
        def _():
            zo = z - step
            te = zo * inner + y
            arrived(te, w)

            @pl.when(z + 1 < outer)
            def _():
                up(slot(te, w), zo).start()

            spread(zo)

        @pl.when(z + step < outer)
        def _():
            zo = z + step
            te = zo * inner + y
            arrived(te, w)

            @pl.when(z > 0)
            def _():
                down(slot(te, w), zo).start()

            spread(zo)

        if inner == 2:
            if step == 1:
                from_across(z)
            else:
                both_sides(step - 1, from_across)
    if inner == 2:
        if outer == 1:
            from_across(z)
        else:
            both_sides(outer - 1, from_across)

    def small(tw):
        extra = xg[pl.ds(pl.multiple_of(tw * wave_rows, wave_rows), wave_rows), width:]
        lanes = extra.shape[1]
        src = lax.broadcasted_iota(jnp.int32, (lanes, LANES), 0)
        col = lax.broadcasted_iota(jnp.int32, (lanes, LANES), 1)
        code_at = 2 * experts
        dest_at = code_at + 2 * books
        is_code = col < books
        pick = jnp.where(is_code & (src == code_at + col), float(RADIX), 0.0)
        pick += jnp.where(is_code & (src == code_at + books + col), 1.0, 0.0)
        pick += jnp.where((col == books) & (src == dest_at), float(RADIX), 0.0)
        pick += jnp.where((col == books) & (src == dest_at + 1), 1.0, 0.0)
        own = e * local + col - (books + 1)
        is_weight = (col > books) & (col <= books + local)
        pick += jnp.where(is_weight & ((src == own) | (src == own + experts)), 1.0, 0.0)
        return dot(extra, pick.astype(BF))

    said = small(w)
    lane = lax.broadcasted_iota(jnp.int32, (wave_rows, shard), 1).astype(F32)
    first = (e * shard).astype(F32)
    for q in range(books):
        mem[:, q * shard:(q + 1) * shard] = jnp.where(
            said[:, q:q + 1] - first == lane, 1.0, 0.0
        ).astype(BF)
    place = lax.broadcasted_iota(jnp.int32, (wave_rows, wave_rows), 1).astype(F32)
    order = jnp.where(said[:, books:books + 1] == place, 1.0, 0.0).astype(BF)
    loads[0].wait()
    f_tile = min(channels, 512)

    @pl.loop(0, channels // f_tile)
    def _(n):
        cols = pl.ds(pl.multiple_of(n * f_tile, f_tile), f_tile)
        part = dot(mem[...], tabv[:, cols]).astype(BF)
        fs[:, cols] = lax.dot_general(
            order, part, (((0,), (0,)), ((), ())), preferred_element_type=F32
        ).astype(BF)

    turns = sorted(range(1, outer), key=lambda d: -min(d, outer - d)) + [0]

    def block(zo, yo):
        return pl.ds(pl.multiple_of((zo * inner + yo) * rows, rows), rows)

    def zrows(zo):
        return pl.ds(pl.multiple_of(zo * rows, rows), rows)

    def y_copy(src, dst, ss, rs, zo):
        return remote(src.at[block(zo, 1 - y), :], dst.at[zrows(zo), :], ss.at[zo], rs.at[zo], ye, w)

    def z_copy(src, dst, ss, rs, d):
        zo = (z + d) % outer
        return remote(src.at[zrows(zo), :], dst.at[zrows(d - 1), :], ss.at[d - 1], rs.at[d - 1], zo * inner + y, w)

    def f_start():
        if inner == 2:
            for d in turns:
                y_copy(fs, fy, fys, fyr, (z + d) % outer).start()

    def f_middle():
        for d in turns:
            zo = (z + d) % outer
            total = fs[block(zo, y), :].astype(F32)
            if inner == 2:
                y_copy(fs, fy, fys, fyr, zo).wait_recv()
                total += fy[zrows(zo), :].astype(F32)
            if d:
                fa[zrows(zo), :] = total.astype(BF)
                z_copy(fa, fz, fzs, fzr, d).start()
            else:
                fr_ref[...] = total

    f_start()

    def chunk(tw, dst):
        x = xg[pl.ds(pl.multiple_of(tw * wave_rows, wave_rows), wave_rows), :width]
        told = small(tw)
        for j in range(local):
            gu = dot(x, wgu[j])
            g = gu[:, :units]
            u = gu[:, units:]
            a = g / (1.0 + jnp.exp(-g)) * u * told[:, books + 1 + j:books + 2 + j]
            act[:, j * units:(j + 1) * units] = a.astype(BF)
        tile = min(width, 512)

        @pl.loop(0, width // tile)
        def _(n):
            cols = pl.ds(pl.multiple_of(n * tile, tile), tile)
            dst[:, cols] = dot(act[...], wdv[:, cols]).astype(BF)

    @pl.loop(0, n_e)
    def _(te):
        arrived(te, peer)

    for load in loads[1:]:
        load.wait()
    chunk(peer, psend)
    swap = remote(psend, precv, p_sem.at[0], p_sem.at[1], e, peer)
    swap.start()
    f_middle()
    chunk(w, pown)
    swap.wait_recv()

    if inner == 2:
        for d in turns:
            zo = (z + d) % outer
            there = block(zo, 1 - y)
            ps[there, :] = (pown[there, :].astype(F32) + precv[there, :].astype(F32)).astype(BF)
            y_copy(ps, my, mys, myr, zo).start()
    mine = None
    for d in turns:
        zo = (z + d) % outer
        here = block(zo, y)
        total = pown[here, :].astype(F32) + precv[here, :].astype(F32)
        if inner == 2:
            y_copy(ps, my, mys, myr, zo).wait_recv()
            total += my[zrows(zo), :].astype(F32)
        if d:
            ma[zrows(zo), :] = total.astype(BF)
            z_copy(ma, mz, mzs, mzr, d).start()
        else:
            mine = total
    for d in turns[:-1]:
        z_copy(fa, fz, fzs, fzr, d).wait_recv()
        fr_ref[...] += fz[zrows(d - 1), :].astype(F32)
    for d in turns[:-1]:
        z_copy(ma, mz, mzs, mzr, d).wait_recv()
        mine += mz[zrows(d - 1), :].astype(F32)
    moe_ref[...] = mine.astype(BF)

    for zo in range(outer):
        @pl.when((z + 1 < outer) & (zo <= z))
        def _():
            up(x_ref, zo).wait_send()

        @pl.when((z > 0) & (zo >= z))
        def _():
            down(x_ref, zo).wait_send()

        if inner == 2:
            across(x_ref, zo).wait_send()
            y_copy(fs, fy, fys, fyr, zo).wait_send()
            y_copy(ps, my, mys, myr, zo).wait_send()
    for d in turns[:-1]:
        z_copy(fa, fz, fzs, fzr, d).wait_send()
        z_copy(ma, mz, mzs, mzr, d).wait_send()

    @pl.loop(0, n_e)
    def _(te):
        over(x_ref, te).wait_send()

    swap.wait_send()


def exchange(packed, w_gate, w_up, w_down, table, width, experts, books):
    n_e = lax.axis_size("expert")
    n_w = lax.axis_size("wave")
    inner = 2 if n_e % 2 == 0 else 1
    outer = n_e // inner
    rows = packed.shape[0]
    local, _, units = w_gate.shape
    channels = table.shape[1]
    wave_rows = n_e * rows
    vm = pltpu.VMEM
    dma = lambda *s: pltpu.SemaphoreType.DMA(s)
    hops = max(outer - 1, 1)
    scratch = [
        vm((n_w * wave_rows, packed.shape[1]), BF),
        vm((local, width, 2 * units), BF),
        vm((local * units, width), BF),
        vm(table.shape, BF),
        vm((wave_rows, table.shape[0]), BF),
        vm((wave_rows, local * units), BF),
        vm((wave_rows, width), BF),
        vm((wave_rows, width), BF),
        vm((wave_rows, width), BF),
        vm((wave_rows, width), BF),
        vm((outer * rows, width), BF),
        vm((outer * rows, width), BF),
        vm((hops * rows, width), BF),
        vm((wave_rows, channels), BF),
        vm((outer * rows, channels), BF),
        vm((outer * rows, channels), BF),
        vm((hops * rows, channels), BF),
        dma(2 + 2 * local), dma(outer), dma(outer), dma(outer), dma(n_e), dma(n_w * n_e),
        dma(2), dma(outer), dma(outer), dma(hops), dma(hops),
        dma(outer), dma(outer), dma(hops), dma(hops),
    ]
    any_spec = pl.BlockSpec(memory_space=pl.ANY)
    vm_spec = pl.BlockSpec(memory_space=pltpu.VMEM)
    return pl.pallas_call(
        functools.partial(kernel, n_e, n_w, inner, experts, books, None),
        out_shape=(
            jax.ShapeDtypeStruct((rows, width), BF),
            jax.ShapeDtypeStruct((rows, channels), F32),
        ),
        in_specs=[vm_spec] + [any_spec] * 4,
        out_specs=(vm_spec, vm_spec),
        scratch_shapes=scratch,
        compiler_params=pltpu.CompilerParams(
            collective_id=0, has_side_effects=True, vmem_limit_bytes=60 * 1024 * 1024
        ),
    )(packed, w_gate, w_up, w_down, table)


def per_device(
    hidden_rows, expert_ids, route_weights, w_gate, w_up, w_down,
    codes, owner_slot, code_table, conv_state, conv_taps, conv_bias, upsample,
):
    n_e = lax.axis_size("expert")
    n_w = lax.axis_size("wave")
    sessions, steps, width = hidden_rows.shape
    rows = sessions * steps
    top = expert_ids.shape[2]
    experts = n_e * w_gate.shape[0]
    books, shard, channels = code_table.shape

    ids = expert_ids.reshape(rows, top)
    names = jnp.arange(experts, dtype=jnp.int32)
    weight = jnp.sum(
        jnp.where(ids[:, :, None] == names, route_weights.reshape(rows, top, 1), 0.0), axis=1
    )
    high = lax.reduce_precision(weight, 8, 7)
    dest = owner_slot // sessions // n_w * sessions + owner_slot % sessions
    dest = (dest[:, None] * steps + jnp.arange(steps, dtype=jnp.int32)).reshape(rows, 1)
    code_rows = codes.reshape(rows, books)
    used = 2 * experts + 2 * books + 2
    extra = jnp.concatenate(
        [
            high.astype(BF),
            (weight - high).astype(BF),
            (code_rows // RADIX).astype(BF),
            (code_rows % RADIX).astype(BF),
            (dest // RADIX).astype(BF),
            (dest % RADIX).astype(BF),
            jnp.zeros((rows, -used % LANES), BF),
        ],
        axis=1,
    )
    packed = jnp.concatenate([hidden_rows.reshape(rows, width), extra], axis=1)
    moe, frames = exchange(
        packed, w_gate, w_up, w_down.reshape(-1, width),
        code_table.reshape(books * shard, channels), width, experts, books,
    )
    frames = frames.reshape(sessions, steps, channels)
    history = jnp.concatenate([conv_state.astype(F32), frames], axis=1)
    state_len = conv_state.shape[1]
    filtered = jnp.broadcast_to(conv_bias, frames.shape)
    for offset in range(conv_taps.shape[0]):
        filtered = filtered + conv_taps[offset] * history[:, state_len - offset:state_len - offset + steps]
    decoded = jax.nn.gelu(filtered).astype(BF)
    samples = jnp.dot(decoded.reshape(rows, channels), upsample, preferred_element_type=F32)
    samples = samples.astype(BF).reshape(sessions, steps, upsample.shape[1])
    carried = history[:, steps:].astype(BF)
    return moe.reshape(sessions, steps, width), samples, carried


def solution(mesh):
    rows = P(("groups", "expert", "wave"), None, None)
    placed = (
        rows, rows, rows,
        P("expert", None, "wave"), P("expert", None, "wave"), P("expert", "wave", None),
        rows, P(("groups", "expert", "wave")), P(None, "expert", None), rows, P(), P(), P(),
    )
    return jax.shard_map(
        per_device, mesh=mesh, in_specs=placed, out_specs=(rows, rows, rows), check_vma=False
    )
```

```python
import functools

import jax
import jax.numpy as jnp
from jax import lax
from jax.experimental import pallas as pl
from jax.experimental.pallas import tpu as pltpu
from jax.sharding import PartitionSpec as P

MESH = pl.DeviceIdType.MESH
BF = jnp.bfloat16
F32 = jnp.float32
RADIX = 64
LANES = 128


def dot(a, b):
    return jnp.dot(a, b, preferred_element_type=F32)


def kernel(
    n_e, n_w, inner, experts, books,
    x_ref, wg_ref, wu_ref, wd_ref, tab_ref,
    moe_ref, fr_ref,
    xg, wgu, wdv, tabv, mem, act,
    part, precv, ps, my, ma, mz,
    fs, fy, fa, fz,
    w_sem, zu_sem, ys_sem, ws_sem, ag_recv,
    p_sem, mys, myr, mzs, mzr, fys, fyr, fzs, fzr,
):
    outer = n_e // inner
    rows = x_ref.shape[0]
    width = moe_ref.shape[1]
    channels = fr_ref.shape[1]
    local = wg_ref.shape[0]
    units = wg_ref.shape[2]
    shard = tab_ref.shape[0] // books
    wave_rows = n_e * rows
    halves = 2 if outer > 1 and outer & (outer - 1) == 0 else 1
    half_e = n_e // halves
    half_rows = half_e * rows
    e = lax.axis_index("expert")
    w = lax.axis_index("wave")
    z = e // inner
    y = e % inner
    peer = 1 - w
    ye = z * inner + (inner - 1 - y)

    def remote(src, dst, ssem, rsem, te, tw):
        return pltpu.make_async_remote_copy(
            src_ref=src, dst_ref=dst, send_sem=ssem, recv_sem=rsem,
            device_id={"expert": te, "wave": tw}, device_id_type=MESH,
        )

    loads = []
    loads.append(pltpu.make_async_copy(tab_ref, tabv, w_sem.at[0]))
    for j in range(local):
        loads.append(pltpu.make_async_copy(wg_ref.at[j], wgu.at[j, :, pl.ds(0, units)], w_sem.at[1 + 2 * j]))
        loads.append(pltpu.make_async_copy(wu_ref.at[j], wgu.at[j, :, pl.ds(units, units)], w_sem.at[2 + 2 * j]))
    loads.append(pltpu.make_async_copy(wd_ref, wdv, w_sem.at[1 + 2 * local]))

    barrier = pltpu.get_barrier_semaphore()

    def greet(te, tw):
        pl.semaphore_signal(barrier, inc=1, device_id={"expert": te, "wave": tw}, device_id_type=MESH)

    power = outer & (outer - 1) == 0

    def far(k):
        if not power:
            return (z + k) % outer, (z - k + outer) % outer
        flipped = z
        bit = 1
        while bit < outer:
            if k & bit:
                flipped = flipped + bit - 2 * bit * (z // bit % 2)
            bit *= 2
        return flipped, flipped

    greet(e, peer)
    if inner == 2:
        greet(ye, w)
    for k in range(1, outer):
        greet(far(k)[0] * inner + y, w)
    pl.semaphore_wait(barrier, 1 + (inner - 1) + (outer - 1))

    def start_row(te, tw):
        return ((te // half_e * n_w + tw) * half_e + te % half_e) * rows

    def slot(te, tw):
        return xg.at[pl.ds(pl.multiple_of(start_row(te, tw), rows), rows), :]

    def along(k):
        return remote(x_ref, slot(e, w), zu_sem.at[k], ag_recv.at[w * n_e + e], far(k)[0] * inner + y, w)

    def across(src, zo):
        te = zo * inner + y
        return remote(src, slot(te, w), ys_sem.at[zo], ag_recv.at[w * n_e + te], ye, w)

    def over(src, te):
        return remote(src, slot(te, w), ws_sem.at[te], ag_recv.at[w * n_e + te], e, peer)

    def arrived(te, tw):
        remote(slot(te, tw), slot(te, tw), ws_sem.at[te], ag_recv.at[tw * n_e + te], e, peer).wait_recv()

    if outer > 1:
        along(1).start()
    if inner == 2:
        across(x_ref, z).start()
    over(x_ref, e).start()
    for k in range(2, outer):
        along(k).start()
    for load in loads:
        load.start()
    xg[pl.ds(pl.multiple_of(start_row(e, w), rows), rows), :] = x_ref[...]

    def spread(k):
        te = far(k)[1] * inner + y
        arrived(te, w)
        if inner == 2:
            across(slot(te, w), far(k)[1]).start()
        over(slot(te, w), te).start()

    def from_across(k):
        if inner == 2:
            te = (far(k)[1] if k else z) * inner + (inner - 1 - y)
            arrived(te, w)
            over(slot(te, w), te).start()

    def wave_half(h):
        @pl.loop(0, half_e)
        def _(i):
            arrived(h * half_e + i, peer)

    def small(extra):
        lanes = extra.shape[1]
        src = lax.broadcasted_iota(jnp.int32, (lanes, LANES), 0)
        col = lax.broadcasted_iota(jnp.int32, (lanes, LANES), 1)
        code_at = 2 * experts
        dest_at = code_at + 2 * books
        is_code = col < books
        pick = jnp.where(is_code & (src == code_at + col), float(RADIX), 0.0)
        pick += jnp.where(is_code & (src == code_at + books + col), 1.0, 0.0)
        pick += jnp.where((col == books) & (src == dest_at), float(RADIX), 0.0)
        pick += jnp.where((col == books) & (src == dest_at + 1), 1.0, 0.0)
        own = e * local + col - (books + 1)
        is_weight = (col > books) & (col <= books + local)
        pick += jnp.where(is_weight & ((src == own) | (src == own + experts)), 1.0, 0.0)
        return dot(extra, pick.astype(BF))

    def frames():
        said = small(jnp.concatenate([
            xg[pl.ds(pl.multiple_of((h * n_w + w) * half_rows, half_rows), half_rows), width:]
            for h in range(halves)
        ], axis=0))
        lane = lax.broadcasted_iota(jnp.int32, (wave_rows, shard), 1).astype(F32)
        first = (e * shard).astype(F32)
        for q in range(books):
            mem[:, q * shard:(q + 1) * shard] = jnp.where(
                said[:, q:q + 1] - first == lane, 1.0, 0.0
            ).astype(BF)
        place = lax.broadcasted_iota(jnp.int32, (wave_rows, wave_rows), 1).astype(F32)
        order = jnp.where(said[:, books:books + 1] == place, 1.0, 0.0).astype(BF)
        loads[0].wait()
        f_tile = min(channels, 512)

        @pl.loop(0, channels // f_tile)
        def _(n):
            cols = pl.ds(pl.multiple_of(n * f_tile, f_tile), f_tile)
            part = dot(mem[...], tabv[:, cols]).astype(BF)
            fs[:, cols] = lax.dot_general(
                order, part, (((0,), (0,)), ((), ())), preferred_element_type=F32
            ).astype(BF)

    turns = list(range(outer - 1, -1, -1))

    def block(zo, yo):
        return pl.ds(pl.multiple_of((zo * inner + yo) * rows, rows), rows)

    def zrows(zo):
        return pl.ds(pl.multiple_of(zo * rows, rows), rows)

    def y_copy(src, dst, ss, rs, zo):
        return remote(src.at[block(zo, 1 - y), :], dst.at[zrows(zo), :], ss.at[zo], rs.at[zo], ye, w)

    def z_copy(src, dst, ss, rs, d):
        zo = far(d)[0] if d else z
        return remote(src.at[zrows(zo), :], dst.at[zrows(d - 1), :], ss.at[d - 1], rs.at[d - 1], zo * inner + y, w)

    def f_start():
        if inner == 2:
            for d in turns:
                y_copy(fs, fy, fys, fyr, far(d)[0] if d else z).start()

    def f_middle():
        for d in turns:
            zo = far(d)[0] if d else z
            total = fs[block(zo, y), :].astype(F32)
            if inner == 2:
                y_copy(fs, fy, fys, fyr, zo).wait_recv()
                total += fy[zrows(zo), :].astype(F32)
            if d:
                fa[zrows(zo), :] = total.astype(BF)
                z_copy(fa, fz, fzs, fzr, d).start()
            else:
                fr_ref[...] = total

    def gate_up(h, j):
        mine = pl.ds(pl.multiple_of(h * (n_w * half_rows), n_w * half_rows), n_w * half_rows)
        told = small(xg[mine, width:])
        if True:
            gu = dot(xg[mine, :width], wgu[j])
            g = gu[:, :units]
            u = gu[:, units:]
            a = g / (1.0 + jnp.exp(-g)) * u * told[:, books + 1 + j:books + 2 + j]
            act[:, j * units:(j + 1) * units] = a.astype(BF)

    def down(h):
        tile = min(width, 512)
        at = [pl.ds(pl.multiple_of((tw * halves + h) * half_rows, half_rows), half_rows) for tw in range(n_w)]

        @pl.loop(0, width // tile)
        def _(n):
            cols = pl.ds(pl.multiple_of(n * tile, tile), tile)
            out = dot(act[...], wdv[:, cols]).astype(BF)
            for tw in range(n_w):
                part[at[tw], cols] = out[tw * half_rows:(tw + 1) * half_rows]

    def swap(h, i):
        rows_out = pl.ds(pl.multiple_of((peer * halves + h) * half_rows, half_rows), half_rows)
        rows_in = pl.ds(pl.multiple_of(h * half_rows, half_rows), half_rows)
        return remote(part.at[rows_out, :], precv.at[rows_in, :], p_sem.at[2 * i], p_sem.at[2 * i + 1], e, peer)

    def paired(zo, yo):
        own = pl.ds(pl.multiple_of(w * wave_rows + (zo * inner + yo) * rows, rows), rows)
        return part[own, :].astype(F32) + precv[block(zo, yo), :].astype(F32)

    def y_start(ks):
        if inner == 2:
            for k in ks:
                zo = far(k)[0] if k else z
                ps[block(zo, 1 - y), :] = paired(zo, 1 - y).astype(BF)
                y_copy(ps, my, mys, myr, zo).start()

    def y_end(k):
        zo = far(k)[0] if k else z
        total = paired(zo, y)
        if inner == 2:
            y_copy(ps, my, mys, myr, zo).wait_recv()
            total += my[zrows(zo), :].astype(F32)
        if k == 0:
            return total
        ma[zrows(zo), :] = total.astype(BF)
        z_copy(ma, mz, mzs, mzr, k).start()

    per_half = outer // halves
    near = list(range(per_half - 1, -1, -1))
    away = list(range(outer - 1, per_half - 1, -1))
    h_near = z // per_half
    h_away = (h_near + 1) % halves
    for k in range(1, per_half):
        spread(k)
        from_across(k - 1)
    if halves == 2:
        spread(per_half)
    from_across(per_half - 1)
    wave_half(h_near)
    for load in loads[1:]:
        load.wait()
    for j in range(local):
        gate_up(h_near, j)
    for k in range(per_half + 1, outer):
        spread(k)
        from_across(k - 1)
    down(h_near)
    swap(h_near, 0).start()
    if halves == 2:
        from_across(outer - 1)
    swap(h_near, 0).wait_recv()
    y_start(near)
    frames()
    f_start()
    if halves == 2:
        wave_half(h_away)
        for j in range(local):
            gate_up(h_away, j)
        down(h_away)
        swap(h_away, 1).start()
    f_middle()
    if halves == 2:
        swap(h_away, 1).wait_recv()
        y_start(away)
    for k in near[:-1] + away:
        y_end(k)
    mine = y_end(0)
    for d in turns[:-1]:
        z_copy(fa, fz, fzs, fzr, d).wait_recv()
        fr_ref[...] += fz[zrows(d - 1), :].astype(F32)
    for d in turns[:-1]:
        z_copy(ma, mz, mzs, mzr, d).wait_recv()
        mine += mz[zrows(d - 1), :].astype(F32)
    moe_ref[...] = mine.astype(BF)

    for zo in range(outer):
        if inner == 2:
            across(x_ref, zo).wait_send()
            y_copy(fs, fy, fys, fyr, zo).wait_send()
            y_copy(ps, my, mys, myr, zo).wait_send()
    for d in turns[:-1]:
        along(d).wait_send()
        z_copy(fa, fz, fzs, fzr, d).wait_send()
        z_copy(ma, mz, mzs, mzr, d).wait_send()

    @pl.loop(0, n_e)
    def _(te):
        over(x_ref, te).wait_send()

    for h in range(halves):
        swap(h_near if h == 0 else h_away, h).wait_send()


def exchange(packed, w_gate, w_up, w_down, table, width, experts, books):
    n_e = lax.axis_size("expert")
    n_w = lax.axis_size("wave")
    inner = 2 if n_e % 2 == 0 else 1
    outer = n_e // inner
    halves = 2 if outer > 1 and outer & (outer - 1) == 0 else 1
    rows = packed.shape[0]
    local, _, units = w_gate.shape
    channels = table.shape[1]
    wave_rows = n_e * rows
    vm = pltpu.VMEM
    dma = lambda *s: pltpu.SemaphoreType.DMA(s)
    hops = max(outer - 1, 1)
    scratch = [
        vm((n_w * wave_rows, packed.shape[1]), BF),
        vm((local, width, 2 * units), BF),
        vm((local * units, width), BF),
        vm(table.shape, BF),
        vm((wave_rows, table.shape[0]), BF),
        vm((n_w * wave_rows // halves, local * units), BF),
        vm((n_w * wave_rows, width), BF),
        vm((wave_rows, width), BF),
        vm((wave_rows, width), BF),
        vm((outer * rows, width), BF),
        vm((outer * rows, width), BF),
        vm((hops * rows, width), BF),
        vm((wave_rows, channels), BF),
        vm((outer * rows, channels), BF),
        vm((outer * rows, channels), BF),
        vm((hops * rows, channels), BF),
        dma(2 + 2 * local), dma(outer), dma(outer), dma(n_e), dma(n_w * n_e),
        dma(4), dma(outer), dma(outer), dma(hops), dma(hops),
        dma(outer), dma(outer), dma(hops), dma(hops),
    ]
    any_spec = pl.BlockSpec(memory_space=pl.ANY)
    vm_spec = pl.BlockSpec(memory_space=pltpu.VMEM)
    return pl.pallas_call(
        functools.partial(kernel, n_e, n_w, inner, experts, books),
        out_shape=(
            jax.ShapeDtypeStruct((rows, width), BF),
            jax.ShapeDtypeStruct((rows, channels), F32),
        ),
        in_specs=[vm_spec] + [any_spec] * 4,
        out_specs=(vm_spec, vm_spec),
        scratch_shapes=scratch,
        compiler_params=pltpu.CompilerParams(
            collective_id=0, has_side_effects=True, vmem_limit_bytes=60 * 1024 * 1024
        ),
    )(packed, w_gate, w_up, w_down, table)


def per_device(
    hidden_rows, expert_ids, route_weights, w_gate, w_up, w_down,
    codes, owner_slot, code_table, conv_state, conv_taps, conv_bias, upsample,
):
    n_e = lax.axis_size("expert")
    n_w = lax.axis_size("wave")
    sessions, steps, width = hidden_rows.shape
    rows = sessions * steps
    top = expert_ids.shape[2]
    experts = n_e * w_gate.shape[0]
    books, shard, channels = code_table.shape

    ids = expert_ids.reshape(rows, top)
    names = jnp.arange(experts, dtype=jnp.int32)
    weight = jnp.sum(
        jnp.where(ids[:, :, None] == names, route_weights.reshape(rows, top, 1), 0.0), axis=1
    )
    high = lax.reduce_precision(weight, 8, 7)
    dest = owner_slot // sessions // n_w * sessions + owner_slot % sessions
    dest = (dest[:, None] * steps + jnp.arange(steps, dtype=jnp.int32)).reshape(rows, 1)
    code_rows = codes.reshape(rows, books)
    used = 2 * experts + 2 * books + 2
    extra = jnp.concatenate(
        [
            high.astype(BF),
            (weight - high).astype(BF),
            (code_rows // RADIX).astype(BF),
            (code_rows % RADIX).astype(BF),
            (dest // RADIX).astype(BF),
            (dest % RADIX).astype(BF),
            jnp.zeros((rows, -used % LANES), BF),
        ],
        axis=1,
    )
    packed = jnp.concatenate([hidden_rows.reshape(rows, width), extra], axis=1)
    moe, frames = exchange(
        packed, w_gate, w_up, w_down.reshape(-1, width),
        code_table.reshape(books * shard, channels), width, experts, books,
    )
    frames = frames.reshape(sessions, steps, channels)
    history = jnp.concatenate([conv_state.astype(F32), frames], axis=1)
    state_len = conv_state.shape[1]
    filtered = jnp.broadcast_to(conv_bias, frames.shape)
    for offset in range(conv_taps.shape[0]):
        filtered = filtered + conv_taps[offset] * history[:, state_len - offset:state_len - offset + steps]
    decoded = jax.nn.gelu(filtered).astype(BF)
    samples = jnp.dot(decoded.reshape(rows, channels), upsample, preferred_element_type=F32)
    samples = samples.astype(BF).reshape(sessions, steps, upsample.shape[1])
    carried = history[:, steps:].astype(BF)
    return moe.reshape(sessions, steps, width), samples, carried


def solution(mesh):
    rows = P(("groups", "expert", "wave"), None, None)
    placed = (
        rows, rows, rows,
        P("expert", None, "wave"), P("expert", None, "wave"), P("expert", "wave", None),
        rows, P(("groups", "expert", "wave")), P(None, "expert", None), rows, P(), P(), P(),
    )
    return jax.shard_map(
        per_device, mesh=mesh, in_specs=placed, out_specs=(rows, rows, rows), check_vma=False
    )
```

```python
import functools

import jax
import jax.numpy as jnp
from jax import lax
from jax.experimental import pallas as pl
from jax.experimental.pallas import tpu as pltpu
from jax.sharding import PartitionSpec as P

MESH = pl.DeviceIdType.MESH
BF = jnp.bfloat16
F32 = jnp.float32
RADIX = 64
LANES = 128


def dot(a, b):
    return jnp.dot(a, b, preferred_element_type=F32)


def kernel(
    n_e, n_w, inner, experts, books,
    h_ref, id_ref, rw_ref, co_ref, ow_ref, st_ref, tap_ref, bias_ref, us_ref,
    wg_ref, wu_ref, wd_ref, tab_ref,
    moe_ref, wave_ref, new_ref,
    stage, early, xg, wgu, wdv, tabv, mem, act,
    psend, precv, pown, ps, my, ma, mz,
    fs, fy, fa, fz, fr_ref,
    w_sem, zu_sem, zd_sem, ys_sem, ws_sem, ag_recv,
    p_sem, mys, myr, mzs, mzr, fys, fyr, fzs, fzr,
):
    outer = n_e // inner
    sessions, steps, width = h_ref.shape
    rows = sessions * steps
    channels = tab_ref.shape[1]
    local = wg_ref.shape[0]
    units = wg_ref.shape[2]
    shard = tab_ref.shape[0] // books
    wave_rows = n_e * rows
    e = lax.axis_index("expert")
    w = lax.axis_index("wave")
    z = e // inner
    y = e % inner
    peer = 1 - w
    ye = z * inner + (inner - 1 - y)

    def remote(src, dst, ssem, rsem, te, tw):
        return pltpu.make_async_remote_copy(
            src_ref=src, dst_ref=dst, send_sem=ssem, recv_sem=rsem,
            device_id={"expert": te, "wave": tw}, device_id_type=MESH,
        )

    loads = []
    loads.append(pltpu.make_async_copy(tab_ref, tabv, w_sem.at[0]))
    for j in range(local):
        loads.append(pltpu.make_async_copy(wg_ref.at[j], wgu.at[j, :, pl.ds(0, units)], w_sem.at[1 + 2 * j]))
        loads.append(pltpu.make_async_copy(wu_ref.at[j], wgu.at[j, :, pl.ds(units, units)], w_sem.at[2 + 2 * j]))
    loads.append(pltpu.make_async_copy(wd_ref, wdv, w_sem.at[1 + 2 * local]))

    lanes = stage.shape[1] - width
    lane_i = lax.broadcasted_iota(jnp.int32, (sessions, lanes), 1)
    eye = lax.broadcasted_iota(jnp.int32, (sessions, sessions), 0) == lax.broadcasted_iota(
        jnp.int32, (sessions, sessions), 1
    )
    owner = jnp.sum(
        jnp.where(eye, jnp.broadcast_to(ow_ref[...].astype(F32), (sessions, sessions)), 0.0),
        axis=1, keepdims=True,
    )
    holder = jnp.floor((owner + 0.5) / sessions)
    within = owner - holder * sessions
    holder = jnp.floor((holder + 0.5) / n_w)
    code_at = 2 * experts
    dest_at = code_at + 2 * books
    hid = h_ref[...]
    for t in range(steps):
        ids = id_ref[:, t, :]
        rw = rw_ref[:, t, :]
        co = co_ref[:, t, :].astype(F32)
        both = jnp.zeros((sessions, lanes), F32)
        for k in range(ids.shape[1]):
            named = ids[:, k:k + 1]
            both += jnp.where((named == lane_i) | (named + experts == lane_i), rw[:, k:k + 1], 0.0)
        high = both.astype(BF).astype(F32)
        extra = jnp.where(lane_i < experts, high, both - high)
        extra = jnp.where(lane_i < code_at, extra, 0.0)
        for q in range(books):
            c = co[:, q:q + 1]
            top = jnp.floor((c + 0.5) / RADIX)
            extra = jnp.where(lane_i == code_at + q, top, extra)
            extra = jnp.where(lane_i == code_at + books + q, c - top * RADIX, extra)
        dest = holder * rows + t * sessions + within
        top = jnp.floor((dest + 0.5) / RADIX)
        extra = jnp.where(lane_i == dest_at, top, extra)
        extra = jnp.where(lane_i == dest_at + 1, dest - top * RADIX, extra)
        stage[t * sessions:(t + 1) * sessions, :width] = hid[:, t, :]
        stage[t * sessions:(t + 1) * sessions, width:] = extra.astype(BF)
    x_ref = stage

    barrier = pltpu.get_barrier_semaphore()

    def greet(te, tw):
        pl.semaphore_signal(barrier, inc=1, device_id={"expert": te, "wave": tw}, device_id_type=MESH)

    greet(e, peer)
    if inner == 2:
        greet(ye, w)
    for d in range(1, outer):
        greet((z + d) % outer * inner + y, w)
    pl.semaphore_wait(barrier, 1 + (inner - 1) + (outer - 1))

    def slot(te, tw):
        return xg.at[pl.ds((tw * n_e + te) * rows, rows), :]

    def up(src, zo):
        te = zo * inner + y
        return remote(src, slot(te, w), zu_sem.at[zo], ag_recv.at[w * n_e + te], (z + 1) * inner + y, w)

    def down(src, zo):
        te = zo * inner + y
        return remote(src, slot(te, w), zd_sem.at[zo], ag_recv.at[w * n_e + te], (z - 1) * inner + y, w)

    def across(src, zo):
        te = zo * inner + y
        return remote(src, slot(te, w), ys_sem.at[zo], ag_recv.at[w * n_e + te], ye, w)

    def over(src, te):
        return remote(src, slot(te, w), ws_sem.at[te], ag_recv.at[w * n_e + te], e, peer)

    def arrived(te, tw):
        remote(slot(te, tw), slot(te, tw), ws_sem.at[te], ag_recv.at[tw * n_e + te], e, peer).wait_recv()

    @pl.when(z + 1 < outer)
    def _():
        up(x_ref, z).start()

    @pl.when(z > 0)
    def _():
        down(x_ref, z).start()

    if inner == 2:
        across(x_ref, z).start()
    over(x_ref, e).start()
    for load in loads:
        load.start()
    xg[pl.ds((w * n_e + e) * rows, rows), :] = x_ref[...]

    state_len = st_ref.shape[1]
    taps = tap_ref.shape[0]
    state = st_ref[...]
    for t in range(steps):
        total = jnp.broadcast_to(bias_ref[...], (sessions, channels))
        for j in range(t + 1, taps):
            total += tap_ref[j:j + 1, :] * state[:, state_len + t - j, :].astype(F32)
        early[t * sessions:(t + 1) * sessions, :] = total
    for i in range(state_len - steps):
        new_ref[:, i, :] = state[:, i + steps, :]

    def spread(zo):
        te = zo * inner + y
        if inner == 2:
            across(slot(te, w), zo).start()
        over(slot(te, w), te).start()

    def from_across(zo):
        te = zo * inner + (inner - 1 - y)
        arrived(te, w)
        over(slot(te, w), te).start()

    def both_sides(step, act_on):
        @pl.when(z - step >= 0)
        def _():
            act_on(z - step)

        @pl.when(z + step < outer)
        def _():
            act_on(z + step)

    for step in range(1, outer):
        @pl.when(z - step >= 0)
        def _():
            zo = z - step
            te = zo * inner + y
            arrived(te, w)

            @pl.when(z + 1 < outer)
            def _():
                up(slot(te, w), zo).start()

            spread(zo)

        @pl.when(z + step < outer)
        def _():
            zo = z + step
            te = zo * inner + y
            arrived(te, w)

            @pl.when(z > 0)
            def _():
                down(slot(te, w), zo).start()

            spread(zo)

        if inner == 2:
            if step == 1:
                from_across(z)
            else:
                both_sides(step - 1, from_across)
    if inner == 2:
        if outer == 1:
            from_across(z)
        else:
            both_sides(outer - 1, from_across)

    def small(tw):
        extra = xg[pl.ds(pl.multiple_of(tw * wave_rows, wave_rows), wave_rows), width:]
        lanes = extra.shape[1]
        src = lax.broadcasted_iota(jnp.int32, (lanes, LANES), 0)
        col = lax.broadcasted_iota(jnp.int32, (lanes, LANES), 1)
        code_at = 2 * experts
        dest_at = code_at + 2 * books
        is_code = col < books
        pick = jnp.where(is_code & (src == code_at + col), float(RADIX), 0.0)
        pick += jnp.where(is_code & (src == code_at + books + col), 1.0, 0.0)
        pick += jnp.where((col == books) & (src == dest_at), float(RADIX), 0.0)
        pick += jnp.where((col == books) & (src == dest_at + 1), 1.0, 0.0)
        own = e * local + col - (books + 1)
        is_weight = (col > books) & (col <= books + local)
        pick += jnp.where(is_weight & ((src == own) | (src == own + experts)), 1.0, 0.0)
        return dot(extra, pick.astype(BF))

    said = small(w)
    lane = lax.broadcasted_iota(jnp.int32, (wave_rows, shard), 1).astype(F32)
    first = (e * shard).astype(F32)
    for q in range(books):
        mem[:, q * shard:(q + 1) * shard] = jnp.where(
            said[:, q:q + 1] - first == lane, 1.0, 0.0
        ).astype(BF)
    place = lax.broadcasted_iota(jnp.int32, (wave_rows, wave_rows), 1).astype(F32)
    order = jnp.where(said[:, books:books + 1] == place, 1.0, 0.0).astype(BF)
    loads[0].wait()
    f_tile = min(channels, 512)

    @pl.loop(0, channels // f_tile)
    def _(n):
        cols = pl.ds(pl.multiple_of(n * f_tile, f_tile), f_tile)
        part = dot(mem[...], tabv[:, cols]).astype(BF)
        fs[:, cols] = lax.dot_general(
            order, part, (((0,), (0,)), ((), ())), preferred_element_type=F32
        ).astype(BF)

    turns = sorted(range(1, outer), key=lambda d: -min(d, outer - d)) + [0]

    def block(zo, yo):
        return pl.ds(pl.multiple_of((zo * inner + yo) * rows, rows), rows)

    def zrows(zo):
        return pl.ds(pl.multiple_of(zo * rows, rows), rows)

    def y_copy(src, dst, ss, rs, zo):
        return remote(src.at[block(zo, 1 - y), :], dst.at[zrows(zo), :], ss.at[zo], rs.at[zo], ye, w)

    def z_copy(src, dst, ss, rs, d):
        zo = (z + d) % outer
        return remote(src.at[zrows(zo), :], dst.at[zrows(d - 1), :], ss.at[d - 1], rs.at[d - 1], zo * inner + y, w)

    def f_start():
        if inner == 2:
            for d in turns:
                y_copy(fs, fy, fys, fyr, (z + d) % outer).start()

    def f_middle():
        for d in turns:
            zo = (z + d) % outer
            total = fs[block(zo, y), :].astype(F32)
            if inner == 2:
                y_copy(fs, fy, fys, fyr, zo).wait_recv()
                total += fy[zrows(zo), :].astype(F32)
            if d:
                fa[zrows(zo), :] = total.astype(BF)
                z_copy(fa, fz, fzs, fzr, d).start()
            else:
                fr_ref[...] = total

    f_start()

    def chunk(tw, dst):
        x = xg[pl.ds(pl.multiple_of(tw * wave_rows, wave_rows), wave_rows), :width]
        told = small(tw)
        for j in range(local):
            gu = dot(x, wgu[j])
            g = gu[:, :units]
            u = gu[:, units:]
            a = g / (1.0 + jnp.exp(-g)) * u * told[:, books + 1 + j:books + 2 + j]
            act[:, j * units:(j + 1) * units] = a.astype(BF)
        tile = min(width, 512)

        @pl.loop(0, width // tile)
        def _(n):
            cols = pl.ds(pl.multiple_of(n * tile, tile), tile)
            dst[:, cols] = dot(act[...], wdv[:, cols]).astype(BF)

    @pl.loop(0, n_e)
    def _(te):
        arrived(te, peer)

    for load in loads[1:]:
        load.wait()
    chunk(peer, psend)
    swap = remote(psend, precv, p_sem.at[0], p_sem.at[1], e, peer)
    swap.start()
    f_middle()
    chunk(w, pown)
    swap.wait_recv()

    if inner == 2:
        for d in turns:
            zo = (z + d) % outer
            there = block(zo, 1 - y)
            ps[there, :] = (pown[there, :].astype(F32) + precv[there, :].astype(F32)).astype(BF)
            y_copy(ps, my, mys, myr, zo).start()
    mine = None
    for d in turns:
        zo = (z + d) % outer
        here = block(zo, y)
        total = pown[here, :].astype(F32) + precv[here, :].astype(F32)
        if inner == 2:
            y_copy(ps, my, mys, myr, zo).wait_recv()
            total += my[zrows(zo), :].astype(F32)
        if d:
            ma[zrows(zo), :] = total.astype(BF)
            z_copy(ma, mz, mzs, mzr, d).start()
        else:
            mine = total
    for d in turns[:-1]:
        z_copy(fa, fz, fzs, fzr, d).wait_recv()
        fr_ref[...] += fz[zrows(d - 1), :].astype(F32)
    got = [fr_ref[t * sessions:(t + 1) * sessions, :] for t in range(steps)]
    decoded = []
    for t in range(steps):
        total = early[t * sessions:(t + 1) * sessions, :]
        for j in range(t + 1):
            total += tap_ref[j:j + 1, :] * got[t - j]
        decoded.append(jax.nn.gelu(total).astype(BF))
        new_ref[:, state_len - steps + t, :] = got[t].astype(BF)
    samples = dot(jnp.concatenate(decoded, axis=0), us_ref[...]).astype(BF)
    for t in range(steps):
        wave_ref[:, t, :] = samples[t * sessions:(t + 1) * sessions]
    for d in turns[:-1]:
        z_copy(ma, mz, mzs, mzr, d).wait_recv()
        mine += mz[zrows(d - 1), :].astype(F32)
    for t in range(steps):
        moe_ref[:, t, :] = mine[t * sessions:(t + 1) * sessions].astype(BF)

    for zo in range(outer):
        @pl.when((z + 1 < outer) & (zo <= z))
        def _():
            up(x_ref, zo).wait_send()

        @pl.when((z > 0) & (zo >= z))
        def _():
            down(x_ref, zo).wait_send()

        if inner == 2:
            across(x_ref, zo).wait_send()
            y_copy(fs, fy, fys, fyr, zo).wait_send()
            y_copy(ps, my, mys, myr, zo).wait_send()
    for d in turns[:-1]:
        z_copy(fa, fz, fzs, fzr, d).wait_send()
        z_copy(ma, mz, mzs, mzr, d).wait_send()

    @pl.loop(0, n_e)
    def _(te):
        over(x_ref, te).wait_send()

    swap.wait_send()


def exchange(small_args, w_gate, w_up, w_down, table, experts, books):
    n_e = lax.axis_size("expert")
    n_w = lax.axis_size("wave")
    inner = 2 if n_e % 2 == 0 else 1
    outer = n_e // inner
    sessions, steps, width = small_args[0].shape
    rows = sessions * steps
    used = 2 * experts + 2 * books + 2
    across = width + used + -used % LANES
    local, _, units = w_gate.shape
    channels = table.shape[1]
    wave_rows = n_e * rows
    vm = pltpu.VMEM
    dma = lambda *s: pltpu.SemaphoreType.DMA(s)
    hops = max(outer - 1, 1)
    scratch = [
        vm((rows, across), BF),
        vm((rows, channels), F32),
        vm((n_w * wave_rows, across), BF),
        vm((local, width, 2 * units), BF),
        vm((local * units, width), BF),
        vm(table.shape, BF),
        vm((wave_rows, table.shape[0]), BF),
        vm((wave_rows, local * units), BF),
        vm((wave_rows, width), BF),
        vm((wave_rows, width), BF),
        vm((wave_rows, width), BF),
        vm((wave_rows, width), BF),
        vm((outer * rows, width), BF),
        vm((outer * rows, width), BF),
        vm((hops * rows, width), BF),
        vm((wave_rows, channels), BF),
        vm((outer * rows, channels), BF),
        vm((outer * rows, channels), BF),
        vm((hops * rows, channels), BF),
        vm((rows, channels), F32),
        dma(2 + 2 * local), dma(outer), dma(outer), dma(outer), dma(n_e), dma(n_w * n_e),
        dma(2), dma(outer), dma(outer), dma(hops), dma(hops),
        dma(outer), dma(outer), dma(hops), dma(hops),
    ]
    any_spec = pl.BlockSpec(memory_space=pl.ANY)
    vm_spec = pl.BlockSpec(memory_space=pltpu.VMEM)
    return pl.pallas_call(
        functools.partial(kernel, n_e, n_w, inner, experts, books),
        out_shape=(
            jax.ShapeDtypeStruct((sessions, steps, width), BF),
            jax.ShapeDtypeStruct((sessions, steps, small_args[8].shape[1]), BF),
            jax.ShapeDtypeStruct(small_args[5].shape, BF),
        ),
        in_specs=[vm_spec] * len(small_args) + [any_spec] * 4,
        out_specs=(vm_spec, vm_spec, vm_spec),
        scratch_shapes=scratch,
        compiler_params=pltpu.CompilerParams(
            collective_id=0, has_side_effects=True, vmem_limit_bytes=60 * 1024 * 1024
        ),
    )(*small_args, w_gate, w_up, w_down, table)


def per_device(
    hidden_rows, expert_ids, route_weights, w_gate, w_up, w_down,
    codes, owner_slot, code_table, conv_state, conv_taps, conv_bias, upsample,
):
    n_e = lax.axis_size("expert")
    width = hidden_rows.shape[2]
    experts = n_e * w_gate.shape[0]
    books, shard, channels = code_table.shape
    return exchange(
        (
            hidden_rows, expert_ids, route_weights, codes, owner_slot.reshape(1, -1),
            conv_state, conv_taps, conv_bias.reshape(1, -1), upsample,
        ),
        w_gate, w_up, w_down.reshape(-1, width), code_table.reshape(books * shard, channels),
        experts, books,
    )


def solution(mesh):
    rows = P(("groups", "expert", "wave"), None, None)
    placed = (
        rows, rows, rows,
        P("expert", None, "wave"), P("expert", None, "wave"), P("expert", "wave", None),
        rows, P(("groups", "expert", "wave")), P(None, "expert", None), rows, P(), P(), P(),
    )
    return jax.shard_map(
        per_device, mesh=mesh, in_specs=placed, out_specs=(rows, rows, rows), check_vma=False
    )
```

```python
import functools

import jax
import jax.numpy as jnp
from jax import lax
from jax.experimental import pallas as pl
from jax.experimental.pallas import tpu as pltpu
from jax.sharding import PartitionSpec as P

MESH = pl.DeviceIdType.MESH
BF = jnp.bfloat16
F32 = jnp.float32
RADIX = 64
LANES = 128


def dot(a, b):
    return jnp.dot(a, b, preferred_element_type=F32)


def kernel(
    n_e, n_w, inner, experts, books,
    h_ref, id_ref, rw_ref, co_ref, ow_ref, st_ref, tap_ref, bias_ref, us_ref,
    wg_ref, wu_ref, wd_ref, tab_ref,
    moe_ref, wave_ref, new_ref,
    stage, early, xg, wgu, wdv, tabv, mem, act,
    psend, precv, pown, ps, my, ma, mz,
    fs, fy, fa, fz, fr_ref,
    w_sem, zu_sem, zd_sem, ys_sem, ws_sem, ag_recv,
    p_sem, mys, myr, mzs, mzr, fys, fyr, fzs, fzr,
):
    outer = n_e // inner
    sessions, steps, width = h_ref.shape
    rows = sessions * steps
    channels = tab_ref.shape[1]
    local = wg_ref.shape[0]
    units = wg_ref.shape[2]
    shard = tab_ref.shape[0] // books
    wave_rows = n_e * rows
    e = lax.axis_index("expert")
    w = lax.axis_index("wave")
    z = e // inner
    y = e % inner
    peer = 1 - w
    ye = z * inner + (inner - 1 - y)

    def remote(src, dst, ssem, rsem, te, tw):
        return pltpu.make_async_remote_copy(
            src_ref=src, dst_ref=dst, send_sem=ssem, recv_sem=rsem,
            device_id={"expert": te, "wave": tw}, device_id_type=MESH,
        )

    loads = []
    loads.append(pltpu.make_async_copy(tab_ref, tabv, w_sem.at[0]))
    for j in range(local):
        loads.append(pltpu.make_async_copy(wg_ref.at[j], wgu.at[j, :, pl.ds(0, units)], w_sem.at[1 + 2 * j]))
        loads.append(pltpu.make_async_copy(wu_ref.at[j], wgu.at[j, :, pl.ds(units, units)], w_sem.at[2 + 2 * j]))
    loads.append(pltpu.make_async_copy(wd_ref, wdv, w_sem.at[1 + 2 * local]))

    lanes = stage.shape[1] - width
    lane_i = lax.broadcasted_iota(jnp.int32, (sessions, lanes), 1)
    eye = lax.broadcasted_iota(jnp.int32, (sessions, sessions), 0) == lax.broadcasted_iota(
        jnp.int32, (sessions, sessions), 1
    )
    lane_f = lane_i.astype(F32)

    def column(row):
        square = jnp.broadcast_to(row.astype(F32), (sessions, sessions))
        return jnp.sum(jnp.where(eye, square, 0.0), axis=1, keepdims=True)

    owner = column(ow_ref[...])
    holder = jnp.floor((owner + 0.5) / sessions)
    within = owner - holder * sessions
    holder = jnp.floor((holder + 0.5) / n_w)
    code_at = 2 * experts
    dest_at = code_at + 2 * books
    hid = h_ref[...]
    for t in range(steps):
        co = co_ref[:, t, :].astype(F32)
        both = jnp.zeros((sessions, lanes), F32)
        for k in range(id_ref.shape[1]):
            named = column(id_ref[t, k:k + 1, :])
            both += jnp.where(
                (named == lane_f) | (named + experts == lane_f), column(rw_ref[t, k:k + 1, :]), 0.0
            )
        high = both.astype(BF).astype(F32)
        extra = jnp.where(lane_i < experts, high, both - high)
        extra = jnp.where(lane_i < code_at, extra, 0.0)
        for q in range(books):
            c = co[:, q:q + 1]
            top = jnp.floor((c + 0.5) / RADIX)
            extra = jnp.where(lane_i == code_at + q, top, extra)
            extra = jnp.where(lane_i == code_at + books + q, c - top * RADIX, extra)
        dest = holder * rows + t * sessions + within
        top = jnp.floor((dest + 0.5) / RADIX)
        extra = jnp.where(lane_i == dest_at, top, extra)
        extra = jnp.where(lane_i == dest_at + 1, dest - top * RADIX, extra)
        stage[t * sessions:(t + 1) * sessions, :width] = hid[:, t, :]
        stage[t * sessions:(t + 1) * sessions, width:] = extra.astype(BF)
    x_ref = stage

    barrier = pltpu.get_barrier_semaphore()

    def greet(te, tw):
        pl.semaphore_signal(barrier, inc=1, device_id={"expert": te, "wave": tw}, device_id_type=MESH)

    greet(e, peer)
    if inner == 2:
        greet(ye, w)
    for d in range(1, outer):
        greet((z + d) % outer * inner + y, w)
    pl.semaphore_wait(barrier, 1 + (inner - 1) + (outer - 1))

    def slot(te, tw):
        return xg.at[pl.ds((tw * n_e + te) * rows, rows), :]

    def up(src, zo):
        te = zo * inner + y
        return remote(src, slot(te, w), zu_sem.at[zo], ag_recv.at[w * n_e + te], (z + 1) * inner + y, w)

    def down(src, zo):
        te = zo * inner + y
        return remote(src, slot(te, w), zd_sem.at[zo], ag_recv.at[w * n_e + te], (z - 1) * inner + y, w)

    def across(src, zo):
        te = zo * inner + y
        return remote(src, slot(te, w), ys_sem.at[zo], ag_recv.at[w * n_e + te], ye, w)

    def over(src, te):
        return remote(src, slot(te, w), ws_sem.at[te], ag_recv.at[w * n_e + te], e, peer)

    def arrived(te, tw):
        remote(slot(te, tw), slot(te, tw), ws_sem.at[te], ag_recv.at[tw * n_e + te], e, peer).wait_recv()

    @pl.when(z + 1 < outer)
    def _():
        up(x_ref, z).start()

    @pl.when(z > 0)
    def _():
        down(x_ref, z).start()

    if inner == 2:
        across(x_ref, z).start()
    over(x_ref, e).start()
    for load in loads:
        load.start()
    xg[pl.ds((w * n_e + e) * rows, rows), :] = x_ref[...]

    state_len = st_ref.shape[0]
    taps = tap_ref.shape[0]
    for t in range(steps):
        total = jnp.broadcast_to(bias_ref[...], (sessions, channels))
        for j in range(t + 1, taps):
            total += tap_ref[j:j + 1, :] * st_ref[state_len + t - j].astype(F32)
        early[t * sessions:(t + 1) * sessions, :] = total
    for i in range(state_len - steps):
        new_ref[i] = st_ref[i + steps]

    def spread(zo):
        te = zo * inner + y
        if inner == 2:
            across(slot(te, w), zo).start()
        over(slot(te, w), te).start()

    def from_across(zo):
        te = zo * inner + (inner - 1 - y)
        arrived(te, w)
        over(slot(te, w), te).start()

    def both_sides(step, act_on):
        @pl.when(z - step >= 0)
        def _():
            act_on(z - step)

        @pl.when(z + step < outer)
        def _():
            act_on(z + step)

    for step in range(1, outer):
        @pl.when(z - step >= 0)
        def _():
            zo = z - step
            te = zo * inner + y
            arrived(te, w)

            @pl.when(z + 1 < outer)
            def _():
                up(slot(te, w), zo).start()

            spread(zo)

        @pl.when(z + step < outer)
        def _():
            zo = z + step
            te = zo * inner + y
            arrived(te, w)

            @pl.when(z > 0)
            def _():
                down(slot(te, w), zo).start()

            spread(zo)

        if inner == 2:
            if step == 1:
                from_across(z)
            else:
                both_sides(step - 1, from_across)
    if inner == 2:
        if outer == 1:
            from_across(z)
        else:
            both_sides(outer - 1, from_across)

    def small(tw):
        extra = xg[pl.ds(pl.multiple_of(tw * wave_rows, wave_rows), wave_rows), width:]
        lanes = extra.shape[1]
        src = lax.broadcasted_iota(jnp.int32, (lanes, LANES), 0)
        col = lax.broadcasted_iota(jnp.int32, (lanes, LANES), 1)
        code_at = 2 * experts
        dest_at = code_at + 2 * books
        is_code = col < books
        pick = jnp.where(is_code & (src == code_at + col), float(RADIX), 0.0)
        pick += jnp.where(is_code & (src == code_at + books + col), 1.0, 0.0)
        pick += jnp.where((col == books) & (src == dest_at), float(RADIX), 0.0)
        pick += jnp.where((col == books) & (src == dest_at + 1), 1.0, 0.0)
        own = e * local + col - (books + 1)
        is_weight = (col > books) & (col <= books + local)
        pick += jnp.where(is_weight & ((src == own) | (src == own + experts)), 1.0, 0.0)
        return dot(extra, pick.astype(BF))

    said = small(w)
    lane = lax.broadcasted_iota(jnp.int32, (wave_rows, shard), 1).astype(F32)
    first = (e * shard).astype(F32)
    for q in range(books):
        mem[:, q * shard:(q + 1) * shard] = jnp.where(
            said[:, q:q + 1] - first == lane, 1.0, 0.0
        ).astype(BF)
    place = lax.broadcasted_iota(jnp.int32, (wave_rows, wave_rows), 1).astype(F32)
    order = jnp.where(said[:, books:books + 1] == place, 1.0, 0.0).astype(BF)
    loads[0].wait()
    f_tile = min(channels, 512)

    @pl.loop(0, channels // f_tile)
    def _(n):
        cols = pl.ds(pl.multiple_of(n * f_tile, f_tile), f_tile)
        part = dot(mem[...], tabv[:, cols]).astype(BF)
        fs[:, cols] = lax.dot_general(
            order, part, (((0,), (0,)), ((), ())), preferred_element_type=F32
        ).astype(BF)

    turns = sorted(range(1, outer), key=lambda d: -min(d, outer - d)) + [0]

    def block(zo, yo):
        return pl.ds(pl.multiple_of((zo * inner + yo) * rows, rows), rows)

    def zrows(zo):
        return pl.ds(pl.multiple_of(zo * rows, rows), rows)

    def y_copy(src, dst, ss, rs, zo):
        return remote(src.at[block(zo, 1 - y), :], dst.at[zrows(zo), :], ss.at[zo], rs.at[zo], ye, w)

    def z_copy(src, dst, ss, rs, d):
        zo = (z + d) % outer
        return remote(src.at[zrows(zo), :], dst.at[zrows(d - 1), :], ss.at[d - 1], rs.at[d - 1], zo * inner + y, w)

    def f_start():
        if inner == 2:
            for d in turns:
                y_copy(fs, fy, fys, fyr, (z + d) % outer).start()

    def f_middle():
        for d in turns:
            zo = (z + d) % outer
            total = fs[block(zo, y), :].astype(F32)
            if inner == 2:
                y_copy(fs, fy, fys, fyr, zo).wait_recv()
                total += fy[zrows(zo), :].astype(F32)
            if d:
                fa[zrows(zo), :] = total.astype(BF)
                z_copy(fa, fz, fzs, fzr, d).start()
            else:
                fr_ref[...] = total

    f_start()

    def chunk(tw, dst):
        x = xg[pl.ds(pl.multiple_of(tw * wave_rows, wave_rows), wave_rows), :width]
        told = small(tw)
        for j in range(local):
            gu = dot(x, wgu[j])
            g = gu[:, :units]
            u = gu[:, units:]
            a = g / (1.0 + jnp.exp(-g)) * u * told[:, books + 1 + j:books + 2 + j]
            act[:, j * units:(j + 1) * units] = a.astype(BF)
        tile = min(width, 512)

        @pl.loop(0, width // tile)
        def _(n):
            cols = pl.ds(pl.multiple_of(n * tile, tile), tile)
            dst[:, cols] = dot(act[...], wdv[:, cols]).astype(BF)

    @pl.loop(0, n_e)
    def _(te):
        arrived(te, peer)

    for load in loads[1:]:
        load.wait()
    chunk(peer, psend)
    swap = remote(psend, precv, p_sem.at[0], p_sem.at[1], e, peer)
    swap.start()
    f_middle()
    chunk(w, pown)
    swap.wait_recv()

    if inner == 2:
        for d in turns:
            zo = (z + d) % outer
            there = block(zo, 1 - y)
            ps[there, :] = (pown[there, :].astype(F32) + precv[there, :].astype(F32)).astype(BF)
            y_copy(ps, my, mys, myr, zo).start()
    mine = None
    for d in turns:
        zo = (z + d) % outer
        here = block(zo, y)
        total = pown[here, :].astype(F32) + precv[here, :].astype(F32)
        if inner == 2:
            y_copy(ps, my, mys, myr, zo).wait_recv()
            total += my[zrows(zo), :].astype(F32)
        if d:
            ma[zrows(zo), :] = total.astype(BF)
            z_copy(ma, mz, mzs, mzr, d).start()
        else:
            mine = total
    for d in turns[:-1]:
        z_copy(fa, fz, fzs, fzr, d).wait_recv()
        fr_ref[...] += fz[zrows(d - 1), :].astype(F32)
    got = [fr_ref[t * sessions:(t + 1) * sessions, :] for t in range(steps)]
    decoded = []
    for t in range(steps):
        total = early[t * sessions:(t + 1) * sessions, :]
        for j in range(t + 1):
            total += tap_ref[j:j + 1, :] * got[t - j]
        decoded.append(jax.nn.gelu(total).astype(BF))
        new_ref[state_len - steps + t] = got[t].astype(BF)
    samples = dot(jnp.concatenate(decoded, axis=0), us_ref[...]).astype(BF)
    for t in range(steps):
        wave_ref[:, t, :] = samples[t * sessions:(t + 1) * sessions]
    for d in turns[:-1]:
        z_copy(ma, mz, mzs, mzr, d).wait_recv()
        mine += mz[zrows(d - 1), :].astype(F32)
    for t in range(steps):
        moe_ref[:, t, :] = mine[t * sessions:(t + 1) * sessions].astype(BF)

    for zo in range(outer):
        @pl.when((z + 1 < outer) & (zo <= z))
        def _():
            up(x_ref, zo).wait_send()

        @pl.when((z > 0) & (zo >= z))
        def _():
            down(x_ref, zo).wait_send()

        if inner == 2:
            across(x_ref, zo).wait_send()
            y_copy(fs, fy, fys, fyr, zo).wait_send()
            y_copy(ps, my, mys, myr, zo).wait_send()
    for d in turns[:-1]:
        z_copy(fa, fz, fzs, fzr, d).wait_send()
        z_copy(ma, mz, mzs, mzr, d).wait_send()

    @pl.loop(0, n_e)
    def _(te):
        over(x_ref, te).wait_send()

    swap.wait_send()


def hand_over(a_ref, b_ref, c_ref, a_out, b_out, c_out):
    a_out[...] = a_ref[...]
    b_out[...] = b_ref[...]
    c_out[...] = c_ref[...]


def exchange(small_args, w_gate, w_up, w_down, table, experts, books):
    n_e = lax.axis_size("expert")
    n_w = lax.axis_size("wave")
    inner = 2 if n_e % 2 == 0 else 1
    outer = n_e // inner
    sessions, steps, width = small_args[0].shape
    rows = sessions * steps
    used = 2 * experts + 2 * books + 2
    across = width + used + -used % LANES
    local, _, units = w_gate.shape
    channels = table.shape[1]
    wave_rows = n_e * rows
    vm = pltpu.VMEM
    dma = lambda *s: pltpu.SemaphoreType.DMA(s)
    hops = max(outer - 1, 1)
    scratch = [
        vm((rows, across), BF),
        vm((rows, channels), F32),
        vm((n_w * wave_rows, across), BF),
        vm((local, width, 2 * units), BF),
        vm((local * units, width), BF),
        vm(table.shape, BF),
        vm((wave_rows, table.shape[0]), BF),
        vm((wave_rows, local * units), BF),
        vm((wave_rows, width), BF),
        vm((wave_rows, width), BF),
        vm((wave_rows, width), BF),
        vm((wave_rows, width), BF),
        vm((outer * rows, width), BF),
        vm((outer * rows, width), BF),
        vm((hops * rows, width), BF),
        vm((wave_rows, channels), BF),
        vm((outer * rows, channels), BF),
        vm((outer * rows, channels), BF),
        vm((hops * rows, channels), BF),
        vm((rows, channels), F32),
        dma(2 + 2 * local), dma(outer), dma(outer), dma(outer), dma(n_e), dma(n_w * n_e),
        dma(2), dma(outer), dma(outer), dma(hops), dma(hops),
        dma(outer), dma(outer), dma(hops), dma(hops),
    ]
    any_spec = pl.BlockSpec(memory_space=pl.ANY)
    vm_spec = pl.BlockSpec(memory_space=pltpu.VMEM)
    return pl.pallas_call(
        functools.partial(kernel, n_e, n_w, inner, experts, books),
        out_shape=(
            jax.ShapeDtypeStruct((sessions, steps, width), BF),
            jax.ShapeDtypeStruct((sessions, steps, small_args[8].shape[1]), BF),
            jax.ShapeDtypeStruct(small_args[5].shape, BF),
        ),
        in_specs=[vm_spec] * len(small_args) + [any_spec] * 4,
        out_specs=(vm_spec, vm_spec, vm_spec),
        scratch_shapes=scratch,
        compiler_params=pltpu.CompilerParams(
            collective_id=0, has_side_effects=True, vmem_limit_bytes=60 * 1024 * 1024
        ),
    )(*small_args, w_gate, w_up, w_down, table)


def per_device(
    hidden_rows, expert_ids, route_weights, w_gate, w_up, w_down,
    codes, owner_slot, code_table, conv_state, conv_taps, conv_bias, upsample,
):
    n_e = lax.axis_size("expert")
    width = hidden_rows.shape[2]
    experts = n_e * w_gate.shape[0]
    books, shard, channels = code_table.shape
    results = exchange(
        (
            hidden_rows, expert_ids.transpose(1, 2, 0), route_weights.transpose(1, 2, 0), codes,
            owner_slot.reshape(1, -1), conv_state.transpose(1, 0, 2), conv_taps, conv_bias.reshape(1, -1), upsample,
        ),
        w_gate, w_up, w_down.reshape(-1, width), code_table.reshape(books * shard, channels),
        experts, books,
    )
    vm_spec = pl.BlockSpec(memory_space=pltpu.VMEM)
    moe, samples, carried = pl.pallas_call(
        hand_over,
        out_shape=tuple(jax.ShapeDtypeStruct(r.shape, r.dtype) for r in results),
        in_specs=[vm_spec] * 3,
        out_specs=(vm_spec,) * 3,
    )(*results)
    return moe, samples, carried.transpose(1, 0, 2)


def solution(mesh):
    rows = P(("groups", "expert", "wave"), None, None)
    placed = (
        rows, rows, rows,
        P("expert", None, "wave"), P("expert", None, "wave"), P("expert", "wave", None),
        rows, P(("groups", "expert", "wave")), P(None, "expert", None), rows, P(), P(), P(),
    )
    return jax.shard_map(
        per_device, mesh=mesh, in_specs=placed, out_specs=(rows, rows, rows), check_vma=False
    )
```
